128 devices in a mesh: frames: 16 (over x, y_lo, core), pairs: 8 (over y_hi, z).
Axes of the slice: x: 4, y: 4 (y_hi: 2, y_lo: 2; y = y_hi * 2 + y_lo), z: 4, core: 2. Of those that a mesh axis runs over, the one named last changes fastest.
Arguments:
- coords: float32 [8192, 3, 384], P('frames'), may hold values from -3 to 3
- pair_first: int32 [512], P('pairs'), may hold values from 0 to 383
- pair_second: int32 [65536], P('pairs'), may hold values from 0 to 383
- enc_weight: bfloat16 [64, 65536], P(None, 'pairs'), may hold values from -0.0234375 to 0.0234375
- enc_bias: float32 [64], replicated, may hold values from -4 to 4
- dec_weight: bfloat16 [64, 65536], P(None, 'pairs'), may hold values from -0.75 to 0.75
- dec_bias: float32 [65536], P('pairs'), may hold values from -3 to 3
- lag_frames: int32 [1], replicated, may hold values from 256 to 512
Outputs:
- grad_enc: float32 [64, 65536], P(None, 'pairs')
- grad_dec: float32 [64, 65536], P(None, 'pairs')
The draws below stay inside these ranges and needn't reach their ends.
Inputs may be any that keep to these rules, and one draw needn't show every extreme that they name: Residue numbers; pair p joins residue pair_first[p // 128] with residue pair_second[p].
All inputs are finite; a program needn't handle non-finite values.
Results may differ from the reference program's by a relative error of at most 0.0003.
Values may be sent and summed in bfloat16 or wider, within the bound.
No kernel may reach another device: no remote copies, remote signals or barrier semaphores. Data moves between devices by JAX's collectives and lax.ppermute only.
A program may use at most 192 MiB of HBM per device.

```python
import math
import jax
import jax.numpy as jnp
from jax import lax

FRAME_DEV = 512
LATENT = 64
RESIDUES = 384
FRAMES = 8192
PAIRS = 65536


def draw_coords(key, part):
    walk_key = jax.random.fold_in(key, 11)
    start_key = jax.random.fold_in(key, 12)
    noise_key = jax.random.fold_in(key, 13)
    reach = 0.45
    unit_step = reach / (math.sqrt(FRAME_DEV) * 37.0)
    half_span = int(1.75 / unit_step)
    coord_unit = 1.75 / half_span
    steps = jax.random.randint(walk_key, (FRAMES, 3, RESIDUES), -64, 65, dtype=jnp.int32)
    start = jax.random.randint(start_key, (1, 3, RESIDUES), 0, 2 * half_span, dtype=jnp.int32)
    walked = jnp.cumsum(steps, axis=0, dtype=jnp.int32) + start
    folded = walked % (2 * half_span)
    tent = half_span - jnp.abs(folded - half_span)
    centered = 2 * tent - half_span
    slow_part = centered.astype(jnp.float32) * coord_unit
    noise = jnp.clip(0.25 * jax.random.normal(noise_key, (FRAMES, 3, RESIDUES), jnp.float32), -1.0, 1.0)
    return (slow_part + noise).astype(jnp.float32)


def plant(values, key, smallest, high):
    place = [jax.random.randint(jax.random.fold_in(key, axis), (), 0, length) for axis, length in enumerate(values.shape)]
    longest = values.shape.index(max(values.shape))
    beside = place[:longest] + [(place[longest] + 1) % values.shape[longest]] + place[longest + 1:]
    return values.at[tuple(place)].set(smallest).at[tuple(beside)].set(high)


def levels(key, shape, shards, low, top_value):
    factor_of = 1.0
    for axis_at, shards_of in shards:
        draws = jax.random.uniform(jax.random.fold_in(jax.random.fold_in(key, 6), axis_at), (shards_of,), jnp.float32, low / len(shards), top_value / len(shards))
        factor_of = factor_of * jnp.repeat(jnp.exp(draws), shape[axis_at] // shards_of).reshape((-1,) + (1,) * (len(shape) - 1 - axis_at))
    return factor_of


def normal_values(rng, extent, scale, limit, cuts=(), kind=jnp.bfloat16):
    values = jax.random.normal(rng, extent, jnp.float32) * scale
    if len(cuts) > 0:
        values = levels(rng, extent, cuts, -0.22, 0.18) * values
    return jnp.clip(values, min=-limit, max=limit).astype(kind)


def setup_inputs(seed: int = 0) -> dict:
    streams_of = jax.random.split(jax.random.key(seed), 9)
    return {
        "coords": draw_coords(jax.random.fold_in(streams_of[8], 71), 0),
        "pair_first": plant(jax.random.randint(streams_of[1], (PAIRS // 128,), 0, RESIDUES), jax.random.fold_in(streams_of[1], 1), 0, RESIDUES - 1).astype(jnp.int32),
        "pair_second": plant(jax.random.randint(streams_of[2], (PAIRS,), 0, RESIDUES), jax.random.fold_in(streams_of[2], 1), 0, RESIDUES - 1).astype(jnp.int32),
        "enc_weight": normal_values(streams_of[3], (LATENT, PAIRS), PAIRS ** -0.5, 0.0234375, ((1, 8),)),
        "enc_bias": normal_values(streams_of[4], (LATENT,), 1.0, 4.0, (), jnp.float32),
        "dec_weight": normal_values(streams_of[5], (LATENT, PAIRS), LATENT ** -0.5, 0.75, ((1, 8),)),
        "dec_bias": normal_values(streams_of[6], (PAIRS,), 0.5, 3.0, ((0, 8),), jnp.float32),
        "lag_frames": jax.random.randint(streams_of[7], (1,), FRAME_DEV // 2, FRAME_DEV + 1).astype(jnp.int32),
    }


cutoff_dist = 2.3
softness = 0.4

def contacts(frame_block, pair_first, pair_second):
    near = jnp.take(frame_block, pair_first, axis=2)
    far = jnp.take(frame_block, pair_second, axis=2)
    far = far.reshape(far.shape[0], 3, pair_first.shape[0], 128)
    offset = far - near[..., None]
    distance = jnp.sqrt(lax.optimization_barrier(jnp.sum(offset * offset, axis=1)))
    value = jax.nn.sigmoid((cutoff_dist - distance) / softness)
    return value.reshape(frame_block.shape[0], -1).astype(jnp.bfloat16)

def reference(coords, pair_first, pair_second, enc_weight, enc_bias, dec_weight, dec_bias, lag_frames):
    shift_now = lag_frames[0]
    padded = jnp.concatenate([coords, jnp.zeros((FRAME_DEV, 3, RESIDUES), coords.dtype)], axis=0)
    block_rows = min(256, FRAME_DEV)
    block_count = FRAMES // block_rows
    scale_factor = 1.0 / jnp.sqrt(jnp.float32(FRAMES) - shift_now.astype(jnp.float32))

    def step(totals, block_idx):
        grad_enc, grad_dec = totals
        begin_row = block_idx * block_rows
        own_coords = lax.dynamic_slice_in_dim(coords, begin_row, block_rows, 0)
        later_coords = lax.dynamic_slice_in_dim(padded, begin_row + shift_now, block_rows, 0)
        contact = contacts(own_coords, pair_first, pair_second)
        target = contacts(later_coords, pair_first, pair_second)
        hidden = lax.dot_general(enc_weight, contact, (((1,), (1,)), ((), ())), preferred_element_type=jnp.float32)
        latent = jnp.tanh(hidden + enc_bias[:, None])
        latent_bf = latent.astype(jnp.bfloat16)
        decoded = lax.dot_general(latent_bf, dec_weight, (((0,), (0,)), ((), ())), preferred_element_type=jnp.float32) + dec_bias[None, :]
        frame_ids = begin_row + jnp.arange(block_rows, dtype=jnp.int32)
        usable = frame_ids + shift_now < FRAMES
        err_bf = jnp.where(usable[:, None], (decoded - target.astype(jnp.float32)) * scale_factor, 0.0).astype(jnp.bfloat16)
        grad_dec = grad_dec + jnp.dot(latent_bf, err_bf, preferred_element_type=jnp.float32)
        backward = lax.dot_general(dec_weight, err_bf, (((1,), (1,)), ((), ())), preferred_element_type=jnp.float32)
        hidden_bf = (backward * (1.0 - latent * latent)).astype(jnp.bfloat16)
        grad_enc = grad_enc + jnp.dot(hidden_bf, contact, preferred_element_type=jnp.float32)
        return ((grad_enc, grad_dec), None)
    zeros = jnp.zeros((LATENT, PAIRS), jnp.float32)
    (grad_enc, grad_dec), unused = lax.scan(step, (zeros, zeros), jnp.arange(block_count, dtype=jnp.int32))
    return (grad_enc, grad_dec)
```

```python
import functools

import jax
import jax.numpy as jnp
from jax import lax
from jax.experimental import pallas as pl
from jax.experimental.pallas import tpu as pltpu
from jax.sharding import PartitionSpec as P


cutoff_dist = 2.3
softness = 0.4
LANES = 128
BF = jnp.bfloat16
F32 = jnp.float32


def params():
    return pltpu.CompilerParams(dimension_semantics=("arbitrary",), vmem_limit_bytes=56 << 20)


def contact_kernel(first_ref, second_ref, coords_ref, enc_ref, contact_ref, sum_ref, table, total, *, width):
    frames = coords_ref.shape[1]
    residues = coords_ref.shape[2]
    block = pl.program_id(0)

    @pl.when(block == 0)
    def _():
        for c in range(3):
            value = coords_ref[c]
            high = value.astype(BF)
            low = (value - high.astype(F32)).astype(BF)
            table[c * frames:(c + 1) * frames, :residues] = high
            table[c * frames:(c + 1) * frames, residues:] = low
        total[...] = jnp.zeros_like(total)

    picks = []
    for g in range(width // LANES):
        rows = lax.broadcasted_iota(jnp.int32, (residues, LANES), 0)
        second = second_ref[:, g * LANES:(g + 1) * LANES]
        first = first_ref[block * (width // LANES) + g]
        far = jnp.where(rows == second, 1.0, 0.0)
        near = jnp.where(rows == first, 1.0, 0.0)
        picks.append((far - near).astype(BF))
    pick = jnp.concatenate(picks, axis=1)
    pick = jnp.concatenate([pick, pick], axis=0)
    offset = jnp.dot(table[...], pick, preferred_element_type=F32)
    x, y, z = (offset[c * frames:(c + 1) * frames] for c in range(3))
    distance = jnp.sqrt(x * x + y * y + z * z)
    contact = jax.nn.sigmoid((cutoff_dist - distance) * (1.0 / softness)).astype(BF)
    contact_ref[...] = contact
    total[...] += lax.dot_general(
        enc_ref[...], contact, (((1,), (1,)), ((), ())), preferred_element_type=F32
    )

    @pl.when(block == pl.num_programs(0) - 1)
    def _():
        sum_ref[...] = total[...]


def contacts_and_sum(coords, first, second, enc, width):
    _, frames, residues = coords.shape
    latents, pairs = enc.shape
    return pl.pallas_call(
        functools.partial(contact_kernel, width=width),
        grid_spec=pltpu.PrefetchScalarGridSpec(
            num_scalar_prefetch=1,
            grid=(pairs // width,),
            in_specs=[
                pl.BlockSpec((1, width), lambda j, s: (0, j)),
                pl.BlockSpec((3, frames, residues), lambda j, s: (0, 0, 0)),
                pl.BlockSpec((latents, width), lambda j, s: (0, j)),
            ],
            out_specs=[
                pl.BlockSpec((frames, width), lambda j, s: (0, j)),
                pl.BlockSpec((latents, frames), lambda j, s: (0, 0)),
            ],
            scratch_shapes=[
                pltpu.VMEM((3 * frames, 2 * residues), BF),
                pltpu.VMEM((latents, frames), F32),
            ],
        ),
        out_shape=[
            jax.ShapeDtypeStruct((frames, pairs), BF),
            jax.ShapeDtypeStruct((latents, frames), F32),
        ],
        compiler_params=params(),
        name="contacts",
    )(first, second.reshape(1, pairs), coords, enc)


def decode_kernel(
    info_ref, scale_ref, latent_ref, before_ref, dec_ref, bias_ref, contact_ref,
    keep_ref, give_ref, back_ref, rolled, rolled_t, scale_col, grad, back,
):
    latents, frames = latent_ref.shape
    lag, is_first, core = info_ref[0], info_ref[1], info_ref[2]
    block = pl.program_id(0)

    @pl.when(block == 0)
    def _():
        own = pltpu.roll(latent_ref[...].astype(F32), lag, 1)
        before = pltpu.roll(before_ref[...].astype(F32), lag, 1)
        frame = lax.broadcasted_iota(jnp.int32, (latents, frames), 1)
        value = jnp.where(frame >= lag, own, before)
        rolled[...] = value.astype(BF)
        rolled_t[...] = value.T.astype(BF)
        row = lax.broadcasted_iota(jnp.int32, (frames, LANES), 0)
        scale_col[...] = jnp.where((row < lag) & (is_first == 1), 0.0, scale_ref[0])
        back[...] = jnp.zeros_like(back)

    dec = dec_ref[...]
    decoded = jnp.dot(rolled_t[...], dec, preferred_element_type=F32) + bias_ref[...]
    width = dec.shape[1]
    scale = jnp.concatenate([scale_col[...]] * (width // LANES), axis=1)
    err = ((decoded - contact_ref[...].astype(F32)) * scale).astype(BF)
    grad[...] = jnp.dot(rolled[...], err, preferred_element_type=F32)
    half = latents // 2
    keep_ref[0] = grad[pl.ds(pl.multiple_of(core * half, 8), half), :]
    give_ref[0] = grad[pl.ds(pl.multiple_of((1 - core) * half, 8), half), :]
    back[...] += lax.dot_general(dec, err, (((1,), (1,)), ((), ())), preferred_element_type=F32)

    @pl.when(block == pl.num_programs(0) - 1)
    def _():
        back_ref[...] = pltpu.roll(back[...], lax.rem(frames - lag, frames), 1)


def piece_of(k, chip):
    x, y = chip // 2, lax.rem(chip, 2)
    return lax.rem(x + k // 2, 4) * 2 + lax.rem(y + lax.rem(k, 2), 2)


def decode(info, scale, latent, before, dec, bias, contact, pieces):
    latents, frames = latent.shape
    pairs = dec.shape[1]
    width = pairs // pieces
    half = latents // 2
    col = lambda j, s, f: (0, piece_of(j, s[3]))
    whole = lambda j, s, f: (0, 0)
    return pl.pallas_call(
        decode_kernel,
        grid_spec=pltpu.PrefetchScalarGridSpec(
            num_scalar_prefetch=2,
            grid=(pieces,),
            in_specs=[
                pl.BlockSpec((latents, frames), whole),
                pl.BlockSpec((latents, frames), whole),
                pl.BlockSpec((latents, width), col),
                pl.BlockSpec((1, width), col),
                pl.BlockSpec((frames, width), col),
            ],
            out_specs=[
                pl.BlockSpec((1, half, width), lambda j, s, f: (j, 0, 0)),
                pl.BlockSpec((1, half, width), lambda j, s, f: (j, 0, 0)),
                pl.BlockSpec((latents, frames), whole),
            ],
            scratch_shapes=[
                pltpu.VMEM((latents, frames), BF),
                pltpu.VMEM((frames, latents), BF),
                pltpu.VMEM((frames, LANES), F32),
                pltpu.VMEM((latents, width), F32),
                pltpu.VMEM((latents, frames), F32),
            ],
        ),
        out_shape=[
            jax.ShapeDtypeStruct((pieces, half, width), F32),
            jax.ShapeDtypeStruct((pieces, half, width), F32),
            jax.ShapeDtypeStruct((latents, frames), F32),
        ],
        compiler_params=params(),
        name="decode",
    )(info, scale, latent, before, dec, bias.reshape(1, pairs), contact)


def encode_kernel(info_ref, hidden_ref, contact_ref, keep_ref, give_ref, grad):
    core = info_ref[2]
    half = hidden_ref.shape[0] // 2
    grad[...] = jnp.dot(hidden_ref[...], contact_ref[...], preferred_element_type=F32)
    keep_ref[0] = grad[pl.ds(pl.multiple_of(core * half, 8), half), :]
    give_ref[0] = grad[pl.ds(pl.multiple_of((1 - core) * half, 8), half), :]


def encode(info, hidden, contact, pieces):
    latents, frames = hidden.shape
    pairs = contact.shape[1]
    width = pairs // pieces
    half = latents // 2
    return pl.pallas_call(
        encode_kernel,
        grid_spec=pltpu.PrefetchScalarGridSpec(
            num_scalar_prefetch=1,
            grid=(pieces,),
            in_specs=[
                pl.BlockSpec((latents, frames), lambda j, s: (0, 0)),
                pl.BlockSpec((frames, width), lambda j, s: (0, piece_of(j, s[3]))),
            ],
            out_specs=[
                pl.BlockSpec((1, half, width), lambda j, s: (j, 0, 0)),
                pl.BlockSpec((1, half, width), lambda j, s: (j, 0, 0)),
            ],
            scratch_shapes=[pltpu.VMEM((latents, width), F32)],
        ),
        out_shape=[jax.ShapeDtypeStruct((pieces, half, width), F32)] * 2,
        compiler_params=params(),
        name="encode",
    )(info, hidden, contact)


def gather_kernel(info_ref, mine_ref, other_ref, out_ref):
    core = info_ref[2]
    half = mine_ref.shape[1]
    out_ref[pl.ds(pl.multiple_of(core * half, 8), half), :] = mine_ref[0]
    out_ref[pl.ds(pl.multiple_of((1 - core) * half, 8), half), :] = other_ref[0]


def assemble(info, mine, other):
    pieces, half, width = mine.shape
    return pl.pallas_call(
        gather_kernel,
        grid_spec=pltpu.PrefetchScalarGridSpec(
            num_scalar_prefetch=1,
            grid=(pieces,),
            in_specs=[
                pl.BlockSpec((1, half, width), lambda j, s: (j, 0, 0)),
                pl.BlockSpec((1, half, width), lambda j, s: (j, 0, 0)),
            ],
            out_specs=pl.BlockSpec((2 * half, width), lambda j, s: (0, piece_of(j, s[3]))),
        ),
        out_shape=jax.ShapeDtypeStruct((2 * half, pieces * width), F32),
        compiler_params=params(),
        name="assemble",
    )(info, mine, other)


def ring_pairs(step):
    if step == 0:
        return [(i, i ^ 4) for i in range(8)]
    near = {0: 1, 1: 0, 2: 3, 3: 2} if step == 1 else {0: 3, 3: 0, 1: 2, 2: 1}
    return [(i, (i // 4) * 4 + near[i % 4]) for i in range(8)]


def sum_over_pairs(value):
    for step in range(3):
        value = value + lax.ppermute(value, "pairs", ring_pairs(step))
    return value


def to_chip(value, k, back=False):
    route = []
    for i in range(16):
        x, y, core = i // 4, (i // 2) % 2, i % 2
        target = ((x + k // 2) % 4) * 4 + (y ^ (k % 2)) * 2 + core
        route.append((target, i) if back else (i, target))
    return lax.ppermute(value, "frames", route)


def swap_cores(value):
    return lax.ppermute(value, "frames", [(i, i ^ 1) for i in range(16)])


def sum_over_frames(keep, give, info):
    pieces = keep.shape[0]
    summed = keep + swap_cores(give)
    total = summed[0]
    for k in range(1, pieces):
        total = total + to_chip(summed[k], k)
    mine = jnp.stack([total] + [to_chip(total, k, back=True) for k in range(1, pieces)])
    return assemble(info, mine, swap_cores(mine))


def local(coords, pair_first, pair_second, enc_weight, enc_bias, dec_weight, dec_bias, lag_frames):
    frame_rows = coords.shape[0]
    devices = lax.axis_size("frames")
    total_frames = frame_rows * devices
    lag = lag_frames[0]
    place = lax.axis_index("frames")
    info = jnp.stack([lag, (place == 0).astype(jnp.int32), place % 2, place // 2]).astype(jnp.int32)
    scale = (1.0 / jnp.sqrt(jnp.float32(total_frames) - lag.astype(F32))).reshape(1)
    pieces = devices // 2

    contact, partial_sum = contacts_and_sum(
        jnp.transpose(coords, (1, 0, 2)), pair_first, pair_second, enc_weight, 512
    )
    latent = jnp.tanh(sum_over_pairs(partial_sum) + enc_bias[:, None])
    latent_bf = latent.astype(BF)
    before = lax.ppermute(latent_bf, "frames", [(i, i + 1) for i in range(devices - 1)])
    keep, give, back_terms = decode(
        info, scale, latent_bf, before, dec_weight, dec_bias, contact, pieces
    )
    rolled_back = sum_over_pairs(back_terms)
    after = lax.ppermute(rolled_back, "frames", [(i + 1, i) for i in range(devices - 1)])
    frame = jnp.arange(frame_rows, dtype=jnp.int32)
    backward = jnp.where((frame < frame_rows - lag)[None, :], rolled_back, after)
    hidden_bf = (backward * (1.0 - latent * latent)).astype(BF)
    grad_dec = sum_over_frames(keep, give, info)
    keep, give = encode(info, hidden_bf, contact, pieces)
    grad_enc = sum_over_frames(keep, give, info)
    return (grad_enc, grad_dec)


def solution(mesh):
    placed = (
        P("frames", None, None),
        P("pairs"),
        P("pairs"),
        P(None, "pairs"),
        P(),
        P(None, "pairs"),
        P("pairs"),
        P(),
    )
    return jax.shard_map(
        local,
        mesh=mesh,
        in_specs=placed,
        out_specs=(P(None, "pairs"), P(None, "pairs")),
        check_vma=False,
    )
```

```python
import functools
import math

import jax
import jax.numpy as jnp
from jax import lax
from jax.experimental import pallas as pl
from jax.experimental.pallas import tpu as pltpu
from jax.sharding import PartitionSpec as P


cutoff_dist = 2.3
softness = 0.4
LANES = 128
BF = jnp.bfloat16
F32 = jnp.float32


def params(mib):
    return pltpu.CompilerParams(dimension_semantics=("arbitrary",), vmem_limit_bytes=mib << 20)


scaling = 1.0 / (softness * math.log(2.0))
CHUNK = 64


def contact_kernel(first_ref, second_ref, coords_ref, enc_ref, contact_ref, sum_ref, table, total):
    frames, residues = coords_ref.shape[1:]
    width = contact_ref.shape[1]
    block = pl.program_id(0)

    @pl.when(block == 0)
    def _():
        for c in range(3):
            value = coords_ref[c] * scaling
            high = value.astype(BF)
            low = (value - high.astype(F32)).astype(BF)
            for i in range(frames // CHUNK):
                rows = slice((3 * i + c) * CHUNK, (3 * i + c + 1) * CHUNK)
                table[rows, :residues] = high[i * CHUNK:(i + 1) * CHUNK]
                table[rows, residues:] = low[i * CHUNK:(i + 1) * CHUNK]
        total[...] = jnp.zeros_like(total)

    picks = []
    for g in range(width // LANES):
        rows = lax.broadcasted_iota(jnp.int32, (residues, LANES), 0)
        second = second_ref[:, g * LANES:(g + 1) * LANES]
        first = first_ref[block * (width // LANES) + g]
        far = jnp.where(rows == second, 1.0, 0.0)
        near = jnp.where(rows == first, 1.0, 0.0)
        picks.append((far - near).astype(BF))
    pick = jnp.concatenate(picks, axis=1)
    pick = jnp.concatenate([pick, pick], axis=0)
    offset = jnp.dot(table[...], pick, preferred_element_type=F32)
    parts = []
    for i in range(frames // CHUNK):
        x, y, z = (offset[(3 * i + c) * CHUNK:(3 * i + c + 1) * CHUNK] for c in range(3))
        square = x * x + y * y + z * z
        distance = square * lax.rsqrt(jnp.maximum(square, 1e-30))
        below = 1.0 + jnp.exp2(distance - cutoff_dist * scaling)
        value = pl.reciprocal(below, approx=True)
        parts.append((value * (2.0 - below * value)).astype(BF))
    contact = jnp.concatenate(parts, axis=0)
    contact_ref[...] = contact
    total[...] += lax.dot_general(
        enc_ref[...], contact, (((1,), (1,)), ((), ())), preferred_element_type=F32
    )

    @pl.when(block == pl.num_programs(0) - 1)
    def _():
        sum_ref[...] = total[...]


def contacts_and_sum(coords, first, second, enc, width):
    _, frames, residues = coords.shape
    latents, pairs = enc.shape
    return pl.pallas_call(
        contact_kernel,
        grid_spec=pltpu.PrefetchScalarGridSpec(
            num_scalar_prefetch=1,
            grid=(pairs // width,),
            in_specs=[
                pl.BlockSpec((1, width), lambda j, s: (0, j)),
                pl.BlockSpec((3, frames, residues), lambda j, s: (0, 0, 0)),
                pl.BlockSpec((latents, width), lambda j, s: (0, j)),
            ],
            out_specs=[
                pl.BlockSpec((frames, width), lambda j, s: (0, j)),
                pl.BlockSpec((latents, frames), lambda j, s: (0, 0)),
            ],
            scratch_shapes=[
                pltpu.VMEM((3 * frames, 2 * residues), BF),
                pltpu.VMEM((latents, frames), F32),
            ],
        ),
        out_shape=[
            jax.ShapeDtypeStruct((frames, pairs), BF),
            jax.ShapeDtypeStruct((latents, frames), F32),
        ],
        compiler_params=params(56),
        name="contacts",
    )(first, second.reshape(1, pairs), coords, enc)


GROUPS = 8


def write_groups(out_ref, grad, chip):
    for k in range(GROUPS):
        row = pl.multiple_of(jnp.bitwise_xor(chip, k) * 8, 8)
        out_ref[k] = grad[pl.ds(row, 8), :]


def decode_kernel(
    info_ref, scale_ref, latent_ref, before_ref, dec_ref, bias_ref, contact_ref,
    keep_ref, give_ref, back_ref, rolled, rolled_t, scale_col, grad, back,
):
    latents, frames = latent_ref.shape
    lag, is_first, chip = info_ref[0], info_ref[1], info_ref[3]
    block, blocks = pl.program_id(0), pl.num_programs(0)

    @pl.when(block == 0)
    def _():
        own = pltpu.roll(latent_ref[...].astype(F32), lag, 1)
        before = pltpu.roll(before_ref[...].astype(F32), lag, 1)
        frame = lax.broadcasted_iota(jnp.int32, (latents, frames), 1)
        value = jnp.where(frame >= lag, own, before)
        rolled[...] = value.astype(BF)
        rolled_t[:, :latents] = value.T.astype(BF)
        column = lax.broadcasted_iota(jnp.int32, (frames, 16), 1)
        rolled_t[:, latents:] = jnp.where(column < 3, 1.0, 0.0).astype(BF)
        row = lax.broadcasted_iota(jnp.int32, (frames, LANES), 0)
        scale_col[...] = jnp.where((row < lag) & (is_first == 1), 0.0, scale_ref[0])
        back[...] = jnp.zeros_like(back)

    dec = dec_ref[...]
    width = dec.shape[1]
    bias = bias_ref[...]
    high = bias.astype(BF).astype(F32)
    middle = (bias - high).astype(BF).astype(F32)
    low = bias - high - middle
    row = lax.broadcasted_iota(jnp.int32, (16, width), 0)
    rows = jnp.where(row == 0, high, jnp.where(row == 1, middle, jnp.where(row == 2, low, 0.0)))
    weights = jnp.concatenate([dec, rows.astype(BF)], axis=0)
    decoded = jnp.dot(rolled_t[...], weights, preferred_element_type=F32)
    scale = jnp.concatenate([scale_col[...]] * (width // LANES), axis=1)
    err = ((decoded - contact_ref[...].astype(F32)) * scale).astype(BF)
    grad[...] = jnp.dot(rolled[...], err, preferred_element_type=F32)

    @pl.when(block < blocks // 2)
    def _():
        write_groups(give_ref, grad, chip)

    @pl.when(block >= blocks // 2)
    def _():
        write_groups(keep_ref, grad, chip)

    back[...] += lax.dot_general(dec, err, (((1,), (1,)), ((), ())), preferred_element_type=F32)

    @pl.when(block == blocks - 1)
    def _():
        back_ref[...] = pltpu.roll(back[...], lax.rem(frames - lag, frames), 1)


def decode(info, scale, latent, before, dec, bias, contact, blocks):
    latents, frames = latent.shape
    pairs = dec.shape[1]
    width = pairs // blocks
    per = blocks // 2
    col = lambda j, s, f: (0, jnp.where(j < per, 1 - s[2], s[2]) * per + lax.rem(j, per))
    whole = lambda j, s, f: (0, 0)
    return pl.pallas_call(
        decode_kernel,
        grid_spec=pltpu.PrefetchScalarGridSpec(
            num_scalar_prefetch=2,
            grid=(blocks,),
            in_specs=[
                pl.BlockSpec((latents, frames), whole),
                pl.BlockSpec((latents, frames), whole),
                pl.BlockSpec((latents, width), col),
                pl.BlockSpec((1, width), col),
                pl.BlockSpec((frames, width), col),
            ],
            out_specs=[
                pl.BlockSpec((GROUPS, 8, width), lambda j, s, f: (0, 0, jnp.maximum(j - per, 0))),
                pl.BlockSpec((GROUPS, 8, width), lambda j, s, f: (0, 0, jnp.minimum(j, per - 1))),
                pl.BlockSpec((latents, frames), whole),
            ],
            scratch_shapes=[
                pltpu.VMEM((latents, frames), BF),
                pltpu.VMEM((frames, latents + 16), BF),
                pltpu.VMEM((frames, LANES), F32),
                pltpu.VMEM((latents, width), F32),
                pltpu.VMEM((latents, frames), F32),
            ],
        ),
        out_shape=[
            jax.ShapeDtypeStruct((GROUPS, 8, pairs // 2), F32),
            jax.ShapeDtypeStruct((GROUPS, 8, pairs // 2), F32),
            jax.ShapeDtypeStruct((latents, frames), F32),
        ],
        compiler_params=params(56),
        name="decode",
    )(info, scale, latent, before, dec, bias.reshape(1, pairs), contact)


def encode_kernel(info_ref, hidden_ref, contact_ref, out_ref, grad):
    grad[...] = jnp.dot(hidden_ref[...], contact_ref[...], preferred_element_type=F32)
    write_groups(out_ref, grad, info_ref[3])


def encode(info, hidden, contact, blocks, other):
    latents, frames = hidden.shape
    half = contact.shape[1] // 2
    width = half // blocks
    return pl.pallas_call(
        encode_kernel,
        grid_spec=pltpu.PrefetchScalarGridSpec(
            num_scalar_prefetch=1,
            grid=(blocks,),
            in_specs=[
                pl.BlockSpec((latents, frames), lambda j, s: (0, 0)),
                pl.BlockSpec(
                    (frames, width),
                    lambda j, s: (0, (1 - s[2] if other else s[2]) * blocks + j),
                ),
            ],
            out_specs=pl.BlockSpec((GROUPS, 8, width), lambda j, s: (0, 0, j)),
            scratch_shapes=[pltpu.VMEM((latents, width), F32)],
        ),
        out_shape=jax.ShapeDtypeStruct((GROUPS, 8, half), F32),
        compiler_params=params(20),
        name="encode_other_half" if other else "encode_own_half",
    )(info, hidden, contact)


def assemble_kernel(layout, info_ref, *refs):
    pieces, out_refs, sems = refs[:-3][-len(layout):], refs[-3:-1], refs[-1]
    core, chip = info_ref[2], info_ref[3]
    half = out_refs[0].shape[1] // 2
    copies = []
    for ref, (mine, first_col, codes) in zip(pieces, layout):
        side = core if mine else 1 - core
        for m, code in enumerate(codes):
            row = pl.multiple_of(jnp.bitwise_xor(chip, code) * 8, 8)
            col = pl.multiple_of(side * half + first_col, LANES)
            for n, out_ref in enumerate(out_refs):
                copies.append(
                    pltpu.make_async_copy(
                        ref.at[m, n],
                        out_ref.at[pl.ds(row, 8), pl.ds(col, ref.shape[3])],
                        sems.at[len(copies)],
                    )
                )
    for copy in copies:
        copy.start()
    for copy in copies:
        copy.wait()


def assemble(info, pieces, layout, shape, begun=()):
    count = 2 * sum(len(codes) for _, _, codes in layout)
    spec = pl.BlockSpec(memory_space=pl.ANY)
    return pl.pallas_call(
        functools.partial(assemble_kernel, layout),
        grid_spec=pltpu.PrefetchScalarGridSpec(
            num_scalar_prefetch=1,
            grid=(1,),
            in_specs=[spec] * (len(begun) + len(pieces)),
            out_specs=[spec] * 2,
            scratch_shapes=[pltpu.SemaphoreType.DMA((count,))],
        ),
        out_shape=[jax.ShapeDtypeStruct(shape, F32)] * 2,
        input_output_aliases={1 + n: n for n in range(len(begun))},
        compiler_params=params(2),
        name="assemble_rest" if begun else "assemble",
    )(info, *begun, *pieces)


GRAY = (0, 2, 3, 1)


def chip_code(place):
    x, y = place // 4, (place // 2) % 2
    return y * 4 + jnp.where((x == 1) | (x == 2), 2, 0) + jnp.where(x >= 2, 1, 0)


def flip(value, bit):
    route = []
    for i in range(16):
        x, y, core = i // 4, (i // 2) % 2, i % 2
        code = (y * 4 + GRAY[x]) ^ bit
        route.append((i, GRAY.index(code % 4) * 4 + (code // 4) * 2 + core))
    return lax.ppermute(value, "frames", route)


def swap_cores(value):
    return lax.ppermute(value, "frames", [(i, i ^ 1) for i in range(16)])


AXIS_OF = {4: 0, 2: 1, 1: 2}


def scatter(kept, got, parts):
    half = kept[0].shape[2]
    shape = (2, 2, 2, 8, half)
    held = []
    for start, stop, order in parts:
        axes = [AXIS_OF[b] for b in order] + [3, 4]
        arrays = [
            (k.reshape(shape)[..., start:stop] + g.reshape(shape)[..., start:stop]).transpose(axes)
            for k, g in zip(kept, got)
        ]
        held.append(jnp.stack(arrays, axis=3))
    for step in range(3):
        sent = []
        for v, (_, _, order) in zip(held, parts):
            sent.append(flip(v[1], order[step]))
        held = [v[0] + s for v, s in zip(held, sent)]
    return held


def gather(held, parts, half, info):
    for step in (2, 1, 0):
        sent = []
        for v, (_, _, order) in zip(held, parts):
            sent.append(flip(v, order[step]))
        if step > 0:
            held = [jnp.stack([v, s]) for v, s in zip(held, sent)]
    early, late = ([], []), ([], [])
    for v, s, (start, stop, order) in zip(held, sent, parts):
        for array, lead in ((v, 0), (s, order[0])):
            codes = tuple(lead + b1 * order[1] + b2 * order[2] for b1 in (0, 1) for b2 in (0, 1))
            array = array.reshape(4, 2, 8, stop - start)
            swapped = swap_cores(array)
            for mine, piece in ((True, array), (False, swapped)):
                pieces, layout = late if lead else early
                pieces.append(piece)
                layout.append((mine, start, codes))
    begun = assemble(info, early[0], tuple(early[1]), (64, 2 * half))
    return assemble(info, late[0], tuple(late[1]), (64, 2 * half), begun)


def small_call(body, outs, *arrays):
    return pl.pallas_call(
        body,
        out_shape=[jax.ShapeDtypeStruct(shape, kind) for shape, kind in outs],
        compiler_params=pltpu.CompilerParams(vmem_limit_bytes=4 << 20),
    )(*arrays)


def add_kernel(a_ref, b_ref, out_ref):
    out_ref[...] = a_ref[...] + b_ref[...]


def add_four_kernel(a_ref, b_ref, c_ref, d_ref, out_ref):
    out_ref[...] = (a_ref[...] + b_ref[...]) + (c_ref[...] + d_ref[...])


def latent_kernel(a_ref, b_ref, c_ref, d_ref, bias_ref, latent_ref, rounded_ref):
    total = (a_ref[...] + b_ref[...]) + (c_ref[...] + d_ref[...])
    latent = jnp.tanh(total + bias_ref[...])
    latent_ref[...] = latent
    rounded_ref[...] = latent.astype(BF)


def hidden_kernel(back_ref, after_ref, latent_ref, last_ref, hidden_ref):
    frame = lax.broadcasted_iota(jnp.int32, back_ref.shape, 1)
    backward = jnp.where(frame < last_ref[...], back_ref[...], after_ref[...])
    latent = latent_ref[...]
    hidden_ref[...] = (backward * (1.0 - latent * latent)).astype(BF)


def terms_over_pairs(value):
    got = lax.ppermute(value, "pairs", [(i, i ^ 4) for i in range(8)])
    (value,) = small_call(add_kernel, [(value.shape, F32)], value, got)
    terms = [value]
    for k in (1, 3, 2):
        route = [(i, (i // 4) * 4 + (i + k) % 4) for i in range(8)]
        terms.append(lax.ppermute(value, "pairs", route))
    return terms


def local(coords, pair_first, pair_second, enc_weight, enc_bias, dec_weight, dec_bias, lag_frames):
    frame_rows = coords.shape[0]
    devices = lax.axis_size("frames")
    total_frames = frame_rows * devices
    lag = lag_frames[0]
    place = lax.axis_index("frames")
    info = jnp.stack([lag, (place == 0).astype(jnp.int32), place % 2, chip_code(place)])
    info = info.astype(jnp.int32)
    scale = (1.0 / jnp.sqrt(jnp.float32(total_frames) - lag.astype(F32))).reshape(1)
    bias = enc_bias[:, None]
    last = (frame_rows - lag).reshape(1, 1)
    pair_first, info, scale, bias, last = lax.optimization_barrier(
        (pair_first, info, scale, bias, last)
    )

    contact, partial_sum = contacts_and_sum(
        jnp.transpose(coords, (1, 0, 2)), pair_first, pair_second, enc_weight, 2048
    )
    whole = partial_sum.shape
    latent, latent_bf = small_call(
        latent_kernel, [(whole, F32), (whole, BF)],
        *terms_over_pairs(partial_sum), bias,
    )
    before = lax.ppermute(latent_bf, "frames", [(i, i + 1) for i in range(devices - 1)])
    dec_keep, give, back_terms = decode(
        info, scale, latent_bf, before, dec_weight, dec_bias, contact, 4
    )
    dec_got = swap_cores(give)
    (rolled_back,) = small_call(add_four_kernel, [(whole, F32)], *terms_over_pairs(back_terms))
    after = lax.ppermute(rolled_back, "frames", [(i + 1, i) for i in range(devices - 1)])
    (hidden_bf,) = small_call(hidden_kernel, [(whole, BF)], rolled_back, after, latent, last)
    give = encode(info, hidden_bf, contact, 2, True)
    got = swap_cores(give)
    keep = encode(info, hidden_bf, contact, 2, False)
    held = scatter([keep, dec_keep], [got, dec_got], PARTS)
    return tuple(gather(held, PARTS, keep.shape[2], info))


PARTS = ((0, 1408, (4, 2, 1)), (1408, 2816, (2, 1, 4)), (2816, 4096, (1, 4, 2)))


def solution(mesh):
    placed = (
        P("frames", None, None),
        P("pairs"),
        P("pairs"),
        P(None, "pairs"),
        P(),
        P(None, "pairs"),
        P("pairs"),
        P(),
    )
    return jax.shard_map(
        local,
        mesh=mesh,
        in_specs=placed,
        out_specs=(P(None, "pairs"), P(None, "pairs")),
        check_vma=False,
    )
```

```python
import functools
import math

import jax
import jax.numpy as jnp
from jax import lax
from jax.experimental import pallas as pl
from jax.experimental.pallas import tpu as pltpu
from jax.sharding import PartitionSpec as P


cutoff_dist = 2.3
softness = 0.4
LANES = 128
BF = jnp.bfloat16
F32 = jnp.float32


def params(mib):
    return pltpu.CompilerParams(dimension_semantics=("arbitrary",), vmem_limit_bytes=mib << 20)


scaling = 1.0 / (softness * math.log(2.0))
CHUNK = 16


def contact_kernel(first_ref, second_ref, coords_ref, enc_ref, contact_ref, sum_ref, table, total):
    frames, residues = coords_ref.shape[1:]
    width = contact_ref.shape[1]
    block = pl.program_id(0)

    @pl.when(block == 0)
    def _():
        for c in range(3):
            value = coords_ref[c] * scaling
            high = value.astype(BF)
            low = (value - high.astype(F32)).astype(BF)
            for i in range(frames // CHUNK):
                rows = slice((3 * i + c) * CHUNK, (3 * i + c + 1) * CHUNK)
                table[rows, :residues] = high[i * CHUNK:(i + 1) * CHUNK]
                table[rows, residues:] = low[i * CHUNK:(i + 1) * CHUNK]
        total[...] = jnp.zeros_like(total)

    picks = []
    for g in range(width // LANES):
        rows = lax.broadcasted_iota(jnp.int32, (residues, LANES), 0)
        second = second_ref[:, g * LANES:(g + 1) * LANES]
        first = first_ref[block * (width // LANES) + g]
        far = jnp.where(rows == second, 1.0, 0.0)
        near = jnp.where(rows == first, 1.0, 0.0)
        picks.append((far - near).astype(BF))
    pick = jnp.concatenate(picks, axis=1)
    pick = jnp.concatenate([pick, pick], axis=0)
    offset = jnp.dot(table[...], pick, preferred_element_type=F32)
    parts = []
    for i in range(frames // CHUNK):
        x, y, z = (offset[(3 * i + c) * CHUNK:(3 * i + c + 1) * CHUNK] for c in range(3))
        square = x * x + y * y + z * z
        distance = square * lax.rsqrt(jnp.maximum(square, 1e-30))
        below = 1.0 + jnp.exp2(distance - cutoff_dist * scaling)
        value = pl.reciprocal(below, approx=True)
        parts.append((value * (2.0 - below * value)).astype(BF))
    contact = jnp.concatenate(parts, axis=0)
    contact_ref[...] = contact
    total[...] += lax.dot_general(
        enc_ref[...], contact, (((1,), (1,)), ((), ())), preferred_element_type=F32
    )

    @pl.when(block == pl.num_programs(0) - 1)
    def _():
        sum_ref[...] = total[...]


def contacts_and_sum(coords, first, second, enc, width):
    _, frames, residues = coords.shape
    latents, pairs = enc.shape
    return pl.pallas_call(
        contact_kernel,
        grid_spec=pltpu.PrefetchScalarGridSpec(
            num_scalar_prefetch=1,
            grid=(pairs // width,),
            in_specs=[
                pl.BlockSpec((1, width), lambda j, s: (0, j)),
                pl.BlockSpec((3, frames, residues), lambda j, s: (0, 0, 0)),
                pl.BlockSpec((latents, width), lambda j, s: (0, j)),
            ],
            out_specs=[
                pl.BlockSpec((frames, width), lambda j, s: (0, j)),
                pl.BlockSpec((latents, frames), lambda j, s: (0, 0)),
            ],
            scratch_shapes=[
                pltpu.VMEM((3 * frames, 2 * residues), BF),
                pltpu.VMEM((latents, frames), F32),
            ],
        ),
        out_shape=[
            jax.ShapeDtypeStruct((frames, pairs), BF),
            jax.ShapeDtypeStruct((latents, frames), F32),
        ],
        compiler_params=params(42),
        name="contacts",
    )(first, second.reshape(1, pairs), coords, enc)


GROUPS = 8


def write_groups(out_ref, grad, chip):
    for k in range(GROUPS):
        row = pl.multiple_of(jnp.bitwise_xor(chip, k) * 8, 8)
        out_ref[k] = grad[pl.ds(row, 8), :]


def decode_kernel(
    info_ref, scale_ref, latent_ref, before_ref, dec_ref, bias_ref, contact_ref,
    keep_ref, give_ref, back_ref, rolled, rolled_t, scale_col, grad, back,
):
    latents, frames = latent_ref.shape
    lag, is_first, chip = info_ref[0], info_ref[1], info_ref[3]
    block, blocks = pl.program_id(0), pl.num_programs(0)

    @pl.when(block == 0)
    def _():
        own = pltpu.roll(latent_ref[...].astype(F32), lag, 1)
        before = pltpu.roll(before_ref[...].astype(F32), lag, 1)
        frame = lax.broadcasted_iota(jnp.int32, (latents, frames), 1)
        value = jnp.where(frame >= lag, own, before)
        rolled[...] = value.astype(BF)
        rolled_t[:, :latents] = value.T.astype(BF)
        column = lax.broadcasted_iota(jnp.int32, (frames, 16), 1)
        rolled_t[:, latents:] = jnp.where(column < 3, 1.0, 0.0).astype(BF)
        row = lax.broadcasted_iota(jnp.int32, (frames, LANES), 0)
        scale_col[...] = jnp.where((row < lag) & (is_first == 1), 0.0, scale_ref[0])
        back[...] = jnp.zeros_like(back)

    dec = dec_ref[...]
    width = dec.shape[1]
    bias = bias_ref[...]
    high = bias.astype(BF).astype(F32)
    middle = (bias - high).astype(BF).astype(F32)
    low = bias - high - middle
    row = lax.broadcasted_iota(jnp.int32, (16, width), 0)
    rows = jnp.where(row == 0, high, jnp.where(row == 1, middle, jnp.where(row == 2, low, 0.0)))
    weights = jnp.concatenate([dec, rows.astype(BF)], axis=0)
    decoded = jnp.dot(rolled_t[...], weights, preferred_element_type=F32)
    scale = jnp.concatenate([scale_col[...]] * (width // LANES), axis=1)
    err = ((decoded - contact_ref[...].astype(F32)) * scale).astype(BF)
    grad[...] = jnp.dot(rolled[...], err, preferred_element_type=F32)

    @pl.when(block < blocks // 2)
    def _():
        write_groups(give_ref, grad, chip)

    @pl.when(block >= blocks // 2)
    def _():
        write_groups(keep_ref, grad, chip)

    back[...] += lax.dot_general(dec, err, (((1,), (1,)), ((), ())), preferred_element_type=F32)

    @pl.when(block == blocks - 1)
    def _():
        back_ref[...] = pltpu.roll(back[...], lax.rem(frames - lag, frames), 1)


def decode(info, scale, latent, before, dec, bias, contact, blocks):
    latents, frames = latent.shape
    pairs = dec.shape[1]
    width = pairs // blocks
    per = blocks // 2
    col = lambda j, s, f: (0, jnp.where(j < per, 1 - s[2], s[2]) * per + lax.rem(j, per))
    whole = lambda j, s, f: (0, 0)
    return pl.pallas_call(
        decode_kernel,
        grid_spec=pltpu.PrefetchScalarGridSpec(
            num_scalar_prefetch=2,
            grid=(blocks,),
            in_specs=[
                pl.BlockSpec((latents, frames), whole),
                pl.BlockSpec((latents, frames), whole),
                pl.BlockSpec((latents, width), col),
                pl.BlockSpec((1, width), col),
                pl.BlockSpec((frames, width), col),
            ],
            out_specs=[
                pl.BlockSpec((GROUPS, 8, width), lambda j, s, f: (0, 0, jnp.maximum(j - per, 0))),
                pl.BlockSpec((GROUPS, 8, width), lambda j, s, f: (0, 0, jnp.minimum(j, per - 1))),
                pl.BlockSpec((latents, frames), whole),
            ],
            scratch_shapes=[
                pltpu.VMEM((latents, frames), BF),
                pltpu.VMEM((frames, latents + 16), BF),
                pltpu.VMEM((frames, LANES), F32),
                pltpu.VMEM((latents, width), F32),
                pltpu.VMEM((latents, frames), F32),
            ],
        ),
        out_shape=[
            jax.ShapeDtypeStruct((GROUPS, 8, pairs // 2), F32),
            jax.ShapeDtypeStruct((GROUPS, 8, pairs // 2), F32),
            jax.ShapeDtypeStruct((latents, frames), F32),
        ],
        compiler_params=params(36),
        name="decode",
    )(info, scale, latent, before, dec, bias.reshape(1, pairs), contact)


def encode_kernel(info_ref, hidden_ref, contact_ref, out_ref, grad):
    grad[...] = jnp.dot(hidden_ref[...], contact_ref[...], preferred_element_type=F32)
    write_groups(out_ref, grad, info_ref[3])


def encode(info, hidden, contact, blocks, other):
    latents, frames = hidden.shape
    half = contact.shape[1] // 2
    width = half // blocks
    return pl.pallas_call(
        encode_kernel,
        grid_spec=pltpu.PrefetchScalarGridSpec(
            num_scalar_prefetch=1,
            grid=(blocks,),
            in_specs=[
                pl.BlockSpec((latents, frames), lambda j, s: (0, 0)),
                pl.BlockSpec(
                    (frames, width),
                    lambda j, s: (0, (1 - s[2] if other else s[2]) * blocks + j),
                ),
            ],
            out_specs=pl.BlockSpec((GROUPS, 8, width), lambda j, s: (0, 0, j)),
            scratch_shapes=[pltpu.VMEM((latents, width), F32)],
        ),
        out_shape=jax.ShapeDtypeStruct((GROUPS, 8, half), F32),
        compiler_params=params(20),
        name="encode_other_half" if other else "encode_own_half",
    )(info, hidden, contact)


def assemble_kernel(layout, info_ref, *refs):
    pieces, out_refs, sems = refs[:-3][-len(layout):], refs[-3:-1], refs[-1]
    core, chip = info_ref[2], info_ref[3]
    half = out_refs[0].shape[1] // 2
    copies = []
    for ref, (mine, first_col, codes) in zip(pieces, layout):
        side = core if mine else 1 - core
        for m, code in enumerate(codes):
            row = pl.multiple_of(jnp.bitwise_xor(chip, code) * 8, 8)
            col = pl.multiple_of(side * half + first_col, LANES)
            for n, out_ref in enumerate(out_refs):
                copies.append(
                    pltpu.make_async_copy(
                        ref.at[m, n],
                        out_ref.at[pl.ds(row, 8), pl.ds(col, ref.shape[3])],
                        sems.at[len(copies)],
                    )
                )
    for copy in copies:
        copy.start()
    for copy in copies:
        copy.wait()


def assemble(info, pieces, layout, shape, begun=()):
    count = 2 * sum(len(codes) for _, _, codes in layout)
    spec = pl.BlockSpec(memory_space=pl.ANY)
    return pl.pallas_call(
        functools.partial(assemble_kernel, layout),
        grid_spec=pltpu.PrefetchScalarGridSpec(
            num_scalar_prefetch=1,
            grid=(1,),
            in_specs=[spec] * (len(begun) + len(pieces)),
            out_specs=[spec] * 2,
            scratch_shapes=[pltpu.SemaphoreType.DMA((count,))],
        ),
        out_shape=[jax.ShapeDtypeStruct(shape, F32)] * 2,
        input_output_aliases={1 + n: n for n in range(len(begun))},
        compiler_params=params(2),
        name="assemble_rest" if begun else "assemble",
    )(info, *begun, *pieces)


GRAY = (0, 2, 3, 1)


def chip_code(place):
    x, y = place // 4, (place // 2) % 2
    return y * 4 + jnp.where((x == 1) | (x == 2), 2, 0) + jnp.where(x >= 2, 1, 0)


def flip(value, bit):
    route = []
    for i in range(16):
        x, y, core = i // 4, (i // 2) % 2, i % 2
        code = (y * 4 + GRAY[x]) ^ bit
        route.append((i, GRAY.index(code % 4) * 4 + (code // 4) * 2 + core))
    return lax.ppermute(value, "frames", route)


def swap_cores(value):
    return lax.ppermute(value, "frames", [(i, i ^ 1) for i in range(16)])


AXIS_OF = {4: 0, 2: 1, 1: 2}


def scatter(kept, got, parts):
    half = kept[0].shape[2]
    shape = (2, 2, 2, 8, half)
    held = []
    for start, stop, order in parts:
        axes = [AXIS_OF[b] for b in order] + [3, 4]
        arrays = [
            (k.reshape(shape)[..., start:stop] + g.reshape(shape)[..., start:stop]).transpose(axes)
            for k, g in zip(kept, got)
        ]
        held.append(jnp.stack(arrays, axis=3))
    for step in range(3):
        sent = []
        for v, (_, _, order) in zip(held, parts):
            sent.append(flip(v[1], order[step]))
        held = [v[0] + s for v, s in zip(held, sent)]
    return held


def gather(held, parts, half, info):
    for step in (2, 1, 0):
        sent = []
        for v, (_, _, order) in zip(held, parts):
            sent.append(flip(v, order[step]))
        if step > 0:
            held = [jnp.stack([v, s]) for v, s in zip(held, sent)]
    early, late = ([], []), ([], [])
    for v, s, (start, stop, order) in zip(held, sent, parts):
        for array, lead in ((v, 0), (s, order[0])):
            codes = tuple(lead + b1 * order[1] + b2 * order[2] for b1 in (0, 1) for b2 in (0, 1))
            array = array.reshape(4, 2, 8, stop - start)
            swapped = swap_cores(array)
            for mine, piece in ((True, array), (False, swapped)):
                pieces, layout = late if lead else early
                pieces.append(piece)
                layout.append((mine, start, codes))
    begun = assemble(info, early[0], tuple(early[1]), (64, 2 * half))
    return assemble(info, late[0], tuple(late[1]), (64, 2 * half), begun)


def small_call(body, outs, *arrays):
    return pl.pallas_call(
        body,
        out_shape=[jax.ShapeDtypeStruct(shape, kind) for shape, kind in outs],
        compiler_params=pltpu.CompilerParams(vmem_limit_bytes=4 << 20),
    )(*arrays)


def add_kernel(a_ref, b_ref, out_ref):
    out_ref[...] = a_ref[...] + b_ref[...]


def select_add_kernel(a_ref, b_ref, c_ref, d_ref, last_ref, out_ref):
    frame = lax.broadcasted_iota(jnp.int32, out_ref.shape, 1)
    own, after = a_ref[...] + b_ref[...], c_ref[...] + d_ref[...]
    out_ref[...] = jnp.where(frame < last_ref[...], own, after)


def latent_kernel(a_ref, b_ref, c_ref, d_ref, bias_ref, latent_ref, rounded_ref):
    total = (a_ref[...] + b_ref[...]) + (c_ref[...] + d_ref[...])
    latents = total.shape[0]
    row, column = (lax.broadcasted_iota(jnp.int32, (latents, latents), n) for n in (0, 1))
    bias = jnp.sum(jnp.where(row == column, bias_ref[...], 0.0), axis=1, keepdims=True)
    latent = jnp.tanh(total + bias)
    latent_ref[...] = latent
    rounded_ref[...] = latent.astype(BF)


def hidden_kernel(a_ref, b_ref, c_ref, d_ref, latent_ref, hidden_ref):
    backward = (a_ref[...] + b_ref[...]) + (c_ref[...] + d_ref[...])
    latent = latent_ref[...]
    hidden_ref[...] = (backward * (1.0 - latent * latent)).astype(BF)


def along_y(value):
    return lax.ppermute(value, "pairs", [(i, i ^ 4) for i in range(8)])


def along_z(value):
    terms = [value]
    for k in (1, 3, 2):
        route = [(i, (i // 4) * 4 + (i + k) % 4) for i in range(8)]
        terms.append(lax.ppermute(value, "pairs", route))
    return terms


def from_next(value, flip_y):
    route = [(f * 8 + (p ^ flip_y), (f - 1) * 8 + p) for f in range(1, 16) for p in range(8)]
    return lax.ppermute(value, ("frames", "pairs"), route)


def local(coords, pair_first, pair_second, enc_weight, enc_bias, dec_weight, dec_bias, lag_frames):
    frame_rows = coords.shape[0]
    devices = lax.axis_size("frames")
    total_frames = frame_rows * devices
    lag = lag_frames[0]
    place = lax.axis_index("frames")
    info = jnp.stack([lag, (place == 0).astype(jnp.int32), place % 2, chip_code(place)])
    info = info.astype(jnp.int32)
    scale = (1.0 / jnp.sqrt(jnp.float32(total_frames) - lag.astype(F32))).reshape(1)
    bias = enc_bias.reshape(1, -1)
    last = (frame_rows - lag).reshape(1, 1)
    pair_first, info, scale, bias, last = lax.optimization_barrier(
        (pair_first, info, scale, bias, last)
    )

    contact, partial_sum = contacts_and_sum(
        jnp.transpose(coords, (1, 0, 2)), pair_first, pair_second, enc_weight, 2048
    )
    whole = partial_sum.shape
    (half_sum,) = small_call(add_kernel, [(whole, F32)], partial_sum, along_y(partial_sum))
    latent, latent_bf = small_call(
        latent_kernel, [(whole, F32), (whole, BF)],
        *along_z(half_sum), bias,
    )
    before = lax.ppermute(latent_bf, "frames", [(i, i + 1) for i in range(devices - 1)])
    dec_keep, give, back_terms = decode(
        info, scale, latent_bf, before, dec_weight, dec_bias, contact, 4
    )
    dec_got = swap_cores(give)
    (half_sum,) = small_call(
        select_add_kernel, [(whole, F32)],
        back_terms, along_y(back_terms),
        from_next(back_terms, 0), from_next(back_terms, 4), last,
    )
    (hidden_bf,) = small_call(hidden_kernel, [(whole, BF)], *along_z(half_sum), latent)
    give = encode(info, hidden_bf, contact, 2, True)
    got = swap_cores(give)
    keep = encode(info, hidden_bf, contact, 2, False)
    held = scatter([keep, dec_keep], [got, dec_got], PARTS)
    return tuple(gather(held, PARTS, keep.shape[2], info))


PARTS = ((0, 1408, (4, 2, 1)), (1408, 2816, (2, 1, 4)), (2816, 4096, (1, 4, 2)))


def solution(mesh):
    placed = (
        P("frames", None, None),
        P("pairs"),
        P("pairs"),
        P(None, "pairs"),
        P(),
        P(None, "pairs"),
        P("pairs"),
        P(),
    )
    return jax.shard_map(
        local,
        mesh=mesh,
        in_specs=placed,
        out_specs=(P(None, "pairs"), P(None, "pairs")),
        check_vma=False,
    )
```

```python
import functools
import math

import jax
import jax.numpy as jnp
from jax import lax
from jax.experimental import pallas as pl
from jax.experimental.pallas import tpu as pltpu
from jax.sharding import PartitionSpec as P


cutoff_dist = 2.3
softness = 0.4
LANES = 128
BF = jnp.bfloat16
F32 = jnp.float32


def params(mib):
    return pltpu.CompilerParams(dimension_semantics=("arbitrary",), vmem_limit_bytes=mib << 20)


scaling = 1.0 / (softness * math.log(2.0))
CHUNK = 16


def contact_kernel(first_ref, second_ref, coords_ref, enc_ref, contact_ref, sum_ref, table, total):
    frames, residues = coords_ref.shape[1:]
    width = contact_ref.shape[1]
    block = pl.program_id(0)

    @pl.when(block == 0)
    def _():
        for c in range(3):
            value = coords_ref[c] * scaling
            high = value.astype(BF)
            low = (value - high.astype(F32)).astype(BF)
            for i in range(frames // CHUNK):
                rows = slice((3 * i + c) * CHUNK, (3 * i + c + 1) * CHUNK)
                table[rows, :residues] = high[i * CHUNK:(i + 1) * CHUNK]
                table[rows, residues:] = low[i * CHUNK:(i + 1) * CHUNK]
        total[...] = jnp.zeros_like(total)

    picks = []
    for g in range(width // LANES):
        rows = lax.broadcasted_iota(jnp.int32, (residues, LANES), 0)
        second = second_ref[:, g * LANES:(g + 1) * LANES]
        first = first_ref[block * (width // LANES) + g]
        far = jnp.where(rows == second, 1.0, 0.0)
        near = jnp.where(rows == first, 1.0, 0.0)
        picks.append((far - near).astype(BF))
    pick = jnp.concatenate(picks, axis=1)
    pick = jnp.concatenate([pick, pick], axis=0)
    offset = jnp.dot(table[...], pick, preferred_element_type=F32)
    parts = []
    for i in range(frames // CHUNK):
        x, y, z = (offset[(3 * i + c) * CHUNK:(3 * i + c + 1) * CHUNK] for c in range(3))
        square = x * x + y * y + z * z
        distance = square * lax.rsqrt(jnp.maximum(square, 1e-30))
        below = 1.0 + jnp.exp2(distance - cutoff_dist * scaling)
        value = pl.reciprocal(below, approx=True)
        parts.append((value * (2.0 - below * value)).astype(BF))
    contact = jnp.concatenate(parts, axis=0)
    contact_ref[...] = contact
    total[...] += lax.dot_general(
        enc_ref[...], contact, (((1,), (1,)), ((), ())), preferred_element_type=F32
    )

    @pl.when(block == pl.num_programs(0) - 1)
    def _():
        sum_ref[...] = total[...]


def contacts_and_sum(coords, first, second, enc, width):
    _, frames, residues = coords.shape
    latents, pairs = enc.shape
    return pl.pallas_call(
        contact_kernel,
        grid_spec=pltpu.PrefetchScalarGridSpec(
            num_scalar_prefetch=1,
            grid=(pairs // width,),
            in_specs=[
                pl.BlockSpec((1, width), lambda j, s: (0, j)),
                pl.BlockSpec((3, frames, residues), lambda j, s: (0, 0, 0)),
                pl.BlockSpec((latents, width), lambda j, s: (0, j)),
            ],
            out_specs=[
                pl.BlockSpec((frames, width), lambda j, s: (0, j)),
                pl.BlockSpec((latents, frames), lambda j, s: (0, 0)),
            ],
            scratch_shapes=[
                pltpu.VMEM((3 * frames, 2 * residues), BF),
                pltpu.VMEM((latents, frames), F32),
            ],
        ),
        out_shape=[
            jax.ShapeDtypeStruct((frames, pairs), BF),
            jax.ShapeDtypeStruct((latents, frames), F32),
        ],
        compiler_params=params(42),
        name="contacts",
    )(first, second.reshape(1, pairs), coords, enc)


GROUPS = 8


def write_groups(out_ref, grad, chip):
    for k in range(GROUPS):
        row = pl.multiple_of(jnp.bitwise_xor(chip, k) * 8, 8)
        out_ref[k] = grad[pl.ds(row, 8), :]


def decode_kernel(
    info_ref, scale_ref, latent_ref, before_ref, dec_ref, bias_ref, contact_ref,
    keep_ref, give_ref, back_ref, rolled, rolled_t, scale_col, grad, back,
):
    latents, frames = latent_ref.shape
    lag, is_first, chip = info_ref[0], info_ref[1], info_ref[3]
    block, blocks = pl.program_id(0), pl.num_programs(0)

    @pl.when(block == 0)
    def _():
        turn = lax.rem(lag, frames)
        own = pltpu.roll(latent_ref[...].astype(F32), turn, 1)
        before = pltpu.roll(before_ref[...].astype(F32), turn, 1)
        frame = lax.broadcasted_iota(jnp.int32, (latents, frames), 1)
        value = jnp.where(frame >= lag, own, before)
        rolled[...] = value.astype(BF)
        rolled_t[:, :latents] = value.T.astype(BF)
        column = lax.broadcasted_iota(jnp.int32, (frames, 16), 1)
        rolled_t[:, latents:] = jnp.where(column < 3, 1.0, 0.0).astype(BF)
        row = lax.broadcasted_iota(jnp.int32, (frames, LANES), 0)
        scale_col[...] = jnp.where((row < lag) & (is_first == 1), 0.0, scale_ref[0])
        back[...] = jnp.zeros_like(back)

    dec = dec_ref[...]
    width = dec.shape[1]
    bias = bias_ref[...]
    high = bias.astype(BF).astype(F32)
    middle = (bias - high).astype(BF).astype(F32)
    low = bias - high - middle
    row = lax.broadcasted_iota(jnp.int32, (16, width), 0)
    rows = jnp.where(row == 0, high, jnp.where(row == 1, middle, jnp.where(row == 2, low, 0.0)))
    weights = jnp.concatenate([dec, rows.astype(BF)], axis=0)
    decoded = jnp.dot(rolled_t[...], weights, preferred_element_type=F32)
    scale = jnp.concatenate([scale_col[...]] * (width // LANES), axis=1)
    err = ((decoded - contact_ref[...].astype(F32)) * scale).astype(BF)
    grad[...] = jnp.dot(rolled[...], err, preferred_element_type=F32)

    @pl.when(block < blocks // 2)
    def _():
        write_groups(give_ref, grad, chip)

    @pl.when(block >= blocks // 2)
    def _():
        write_groups(keep_ref, grad, chip)

    back[...] += lax.dot_general(dec, err, (((1,), (1,)), ((), ())), preferred_element_type=F32)

    @pl.when(block == blocks - 1)
    def _():
        back_ref[...] = pltpu.roll(back[...], lax.rem(frames - lag, frames), 1)


def decode(info, scale, latent, before, dec, bias, contact, blocks):
    latents, frames = latent.shape
    pairs = dec.shape[1]
    width = pairs // blocks
    per = blocks // 2
    col = lambda j, s, f: (0, jnp.where(j < per, 1 - s[2], s[2]) * per + lax.rem(j, per))
    whole = lambda j, s, f: (0, 0)
    return pl.pallas_call(
        decode_kernel,
        grid_spec=pltpu.PrefetchScalarGridSpec(
            num_scalar_prefetch=2,
            grid=(blocks,),
            in_specs=[
                pl.BlockSpec((latents, frames), whole),
                pl.BlockSpec((latents, frames), whole),
                pl.BlockSpec((latents, width), col),
                pl.BlockSpec((1, width), col),
                pl.BlockSpec((frames, width), col),
            ],
            out_specs=[
                pl.BlockSpec((GROUPS, 8, width), lambda j, s, f: (0, 0, jnp.maximum(j - per, 0))),
                pl.BlockSpec((GROUPS, 8, width), lambda j, s, f: (0, 0, jnp.minimum(j, per - 1))),
                pl.BlockSpec((latents, frames), whole),
            ],
            scratch_shapes=[
                pltpu.VMEM((latents, frames), BF),
                pltpu.VMEM((frames, latents + 16), BF),
                pltpu.VMEM((frames, LANES), F32),
                pltpu.VMEM((latents, width), F32),
                pltpu.VMEM((latents, frames), F32),
            ],
        ),
        out_shape=[
            jax.ShapeDtypeStruct((GROUPS, 8, pairs // 2), F32),
            jax.ShapeDtypeStruct((GROUPS, 8, pairs // 2), F32),
            jax.ShapeDtypeStruct((latents, frames), F32),
        ],
        compiler_params=params(36),
        name="decode",
    )(info, scale, latent, before, dec, bias.reshape(1, pairs), contact)


def encode_kernel(info_ref, hidden_ref, contact_ref, out_ref, grad):
    grad[...] = jnp.dot(hidden_ref[...], contact_ref[...], preferred_element_type=F32)
    write_groups(out_ref, grad, info_ref[3])


def encode(info, hidden, contact, blocks, other):
    latents, frames = hidden.shape
    half = contact.shape[1] // 2
    width = half // blocks
    return pl.pallas_call(
        encode_kernel,
        grid_spec=pltpu.PrefetchScalarGridSpec(
            num_scalar_prefetch=1,
            grid=(blocks,),
            in_specs=[
                pl.BlockSpec((latents, frames), lambda j, s: (0, 0)),
                pl.BlockSpec(
                    (frames, width),
                    lambda j, s: (0, (1 - s[2] if other else s[2]) * blocks + j),
                ),
            ],
            out_specs=pl.BlockSpec((GROUPS, 8, width), lambda j, s: (0, 0, j)),
            scratch_shapes=[pltpu.VMEM((latents, width), F32)],
        ),
        out_shape=jax.ShapeDtypeStruct((GROUPS, 8, half), F32),
        compiler_params=params(20),
        name="encode_other_half" if other else "encode_own_half",
    )(info, hidden, contact)


def assemble_kernel(layout, info_ref, *refs):
    pieces, out_refs, sems = refs[:-3][-len(layout):], refs[-3:-1], refs[-1]
    core, chip = info_ref[2], info_ref[3]
    half = out_refs[0].shape[1] // 2
    copies = []
    for ref, (mine, first_col, codes) in zip(pieces, layout):
        side = core if mine else 1 - core
        for m, code in enumerate(codes):
            row = pl.multiple_of(jnp.bitwise_xor(chip, code) * 8, 8)
            col = pl.multiple_of(side * half + first_col, LANES)
            for n, out_ref in enumerate(out_refs):
                copies.append(
                    pltpu.make_async_copy(
                        ref.at[m, n],
                        out_ref.at[pl.ds(row, 8), pl.ds(col, ref.shape[3])],
                        sems.at[len(copies)],
                    )
                )
    for copy in copies:
        copy.start()
    for copy in copies:
        copy.wait()


def assemble(info, pieces, layout, shape, begun=()):
    count = 2 * sum(len(codes) for _, _, codes in layout)
    spec = pl.BlockSpec(memory_space=pl.ANY)
    return pl.pallas_call(
        functools.partial(assemble_kernel, layout),
        grid_spec=pltpu.PrefetchScalarGridSpec(
            num_scalar_prefetch=1,
            grid=(1,),
            in_specs=[spec] * (len(begun) + len(pieces)),
            out_specs=[spec] * 2,
            scratch_shapes=[pltpu.SemaphoreType.DMA((count,))],
        ),
        out_shape=[jax.ShapeDtypeStruct(shape, F32)] * 2,
        input_output_aliases={1 + n: n for n in range(len(begun))},
        compiler_params=params(2),
        name="assemble_rest" if begun else "assemble",
    )(info, *begun, *pieces)


GRAY = (0, 2, 3, 1)


def chip_code(place):
    x, y = place // 4, (place // 2) % 2
    return y * 4 + jnp.where((x == 1) | (x == 2), 2, 0) + jnp.where(x >= 2, 1, 0)


def flip(value, bit):
    route = []
    for i in range(16):
        x, y, core = i // 4, (i // 2) % 2, i % 2
        code = (y * 4 + GRAY[x]) ^ bit
        route.append((i, GRAY.index(code % 4) * 4 + (code // 4) * 2 + core))
    return lax.ppermute(value, "frames", route)


def swap_cores(value):
    return lax.ppermute(value, "frames", [(i, i ^ 1) for i in range(16)])


AXIS_OF = {4: 0, 2: 1, 1: 2}


def scatter(kept, got, parts):
    half = kept[0].shape[2]
    shape = (2, 2, 2, 8, half)
    held = []
    for start, stop, order in parts:
        axes = [AXIS_OF[b] for b in order] + [3, 4]
        arrays = [
            (k.reshape(shape)[..., start:stop] + g.reshape(shape)[..., start:stop]).transpose(axes)
            for k, g in zip(kept, got)
        ]
        held.append(jnp.stack(arrays, axis=3))
    for step in range(3):
        sent = []
        for v, (_, _, order) in zip(held, parts):
            sent.append(flip(v[1], order[step]))
        held = [v[0] + s for v, s in zip(held, sent)]
    return held


def gather(held, parts, half, info):
    for step in (2, 1, 0):
        sent = []
        for v, (_, _, order) in zip(held, parts):
            sent.append(flip(v, order[step]))
        if step > 0:
            held = [jnp.stack([v, s]) for v, s in zip(held, sent)]
    early, late = ([], []), ([], [])
    for v, s, (start, stop, order) in zip(held, sent, parts):
        for array, lead in ((v, 0), (s, order[0])):
            codes = tuple(lead + b1 * order[1] + b2 * order[2] for b1 in (0, 1) for b2 in (0, 1))
            array = array.reshape(4, 2, 8, stop - start)
            swapped = swap_cores(array)
            for mine, piece in ((True, array), (False, swapped)):
                pieces, layout = late if lead else early
                pieces.append(piece)
                layout.append((mine, start, codes))
    begun = assemble(info, early[0], tuple(early[1]), (64, 2 * half))
    return assemble(info, late[0], tuple(late[1]), (64, 2 * half), begun)


def small_call(body, outs, *arrays):
    return pl.pallas_call(
        body,
        out_shape=[jax.ShapeDtypeStruct(shape, kind) for shape, kind in outs],
        compiler_params=pltpu.CompilerParams(vmem_limit_bytes=4 << 20),
    )(*arrays)


def add_kernel(a_ref, b_ref, out_ref):
    out_ref[...] = a_ref[...] + b_ref[...]


def select_add_kernel(a_ref, b_ref, c_ref, d_ref, last_ref, out_ref):
    frame = lax.broadcasted_iota(jnp.int32, out_ref.shape, 1)
    own, after = a_ref[...] + b_ref[...], c_ref[...] + d_ref[...]
    out_ref[...] = jnp.where(frame < last_ref[...], own, after)


def latent_kernel(a_ref, b_ref, c_ref, d_ref, bias_ref, latent_ref, rounded_ref):
    total = (a_ref[...] + b_ref[...]) + (c_ref[...] + d_ref[...])
    latents = total.shape[0]
    row, column = (lax.broadcasted_iota(jnp.int32, (latents, latents), n) for n in (0, 1))
    bias = jnp.sum(jnp.where(row == column, bias_ref[...], 0.0), axis=1, keepdims=True)
    latent = jnp.tanh(total + bias)
    latent_ref[...] = latent
    rounded_ref[...] = latent.astype(BF)


def hidden_kernel(a_ref, b_ref, c_ref, d_ref, latent_ref, hidden_ref):
    backward = (a_ref[...] + b_ref[...]) + (c_ref[...] + d_ref[...])
    latent = latent_ref[...]
    hidden_ref[...] = (backward * (1.0 - latent * latent)).astype(BF)


def along_y(value):
    return lax.ppermute(value, "pairs", [(i, i ^ 4) for i in range(8)])


def along_z(value):
    terms = [value]
    for k in (1, 3, 2):
        route = [(i, (i // 4) * 4 + (i + k) % 4) for i in range(8)]
        terms.append(lax.ppermute(value, "pairs", route))
    return terms


def from_next(value, flip_y):
    route = [(f * 8 + (p ^ flip_y), (f - 1) * 8 + p) for f in range(1, 16) for p in range(8)]
    return lax.ppermute(value, ("frames", "pairs"), route)


def local(coords, pair_first, pair_second, enc_weight, enc_bias, dec_weight, dec_bias, lag_frames):
    frame_rows = coords.shape[0]
    devices = lax.axis_size("frames")
    total_frames = frame_rows * devices
    lag = lag_frames[0]
    place = lax.axis_index("frames")
    info = jnp.stack([lag, (place == 0).astype(jnp.int32), place % 2, chip_code(place)])
    info = info.astype(jnp.int32)
    scale = (1.0 / jnp.sqrt(jnp.float32(total_frames) - lag.astype(F32))).reshape(1)
    bias = enc_bias.reshape(1, -1)
    last = (frame_rows - lag).reshape(1, 1)
    pair_first, info, scale, bias, last = lax.optimization_barrier(
        (pair_first, info, scale, bias, last)
    )

    contact, partial_sum = contacts_and_sum(
        jnp.transpose(coords, (1, 0, 2)), pair_first, pair_second, enc_weight, 2048
    )
    whole = partial_sum.shape
    (half_sum,) = small_call(add_kernel, [(whole, F32)], partial_sum, along_y(partial_sum))
    latent, latent_bf = small_call(
        latent_kernel, [(whole, F32), (whole, BF)],
        *along_z(half_sum), bias,
    )
    before = lax.ppermute(latent_bf, "frames", [(i, i + 1) for i in range(devices - 1)])
    dec_keep, give, back_terms = decode(
        info, scale, latent_bf, before, dec_weight, dec_bias, contact, 4
    )
    dec_got = swap_cores(give)
    (half_sum,) = small_call(
        select_add_kernel, [(whole, F32)],
        back_terms, along_y(back_terms),
        from_next(back_terms, 0), from_next(back_terms, 4), last,
    )
    (hidden_bf,) = small_call(hidden_kernel, [(whole, BF)], *along_z(half_sum), latent)
    give = encode(info, hidden_bf, contact, 2, True)
    got = swap_cores(give)
    keep = encode(info, hidden_bf, contact, 2, False)
    held = scatter([keep, dec_keep], [got, dec_got], PARTS)
    return tuple(gather(held, PARTS, keep.shape[2], info))


PARTS = ((0, 1408, (4, 2, 1)), (1408, 2816, (2, 1, 4)), (2816, 4096, (1, 4, 2)))


def solution(mesh):
    placed = (
        P("frames", None, None),
        P("pairs"),
        P("pairs"),
        P(None, "pairs"),
        P(),
        P(None, "pairs"),
        P("pairs"),
        P(),
    )
    return jax.shard_map(
        local,
        mesh=mesh,
        in_specs=placed,
        out_specs=(P(None, "pairs"), P(None, "pairs")),
        check_vma=False,
    )
```
